32 devices in a mesh: dp: 4 (over x, core), shard: 8 (over z, y).
Axes of the slice: x: 2, y: 2, z: 4, core: 2. Of those that a mesh axis runs over, the one named last changes fastest.
Arguments:
- table: float32 [16384, 128], P('shard'), may hold values from -6 to 6
- cross_weight: bfloat16 [1024, 1024], replicated, may hold values from -0.1875 to 0.1875
- cross_bias: float32 [1024], replicated, may hold values from -3 to 3
- top_weight: bfloat16 [1024, 512], replicated, may hold values from -0.1875 to 0.1875
- top_bias: float32 [512], replicated, may hold values from -3 to 3
- out_weight: float32 [512], replicated, may hold values from -0.25 to 0.25
- wanted: int32 [32, 8, 128], P(('dp', 'shard')), may hold values from 0 to 2047, as said below
- slots: int32 [16384, 8, 4], P(('dp', 'shard')), may hold values from 0 to 1023
- lengths: int32 [16384, 8], P(('dp', 'shard')), may hold values from 1 to 4
- logit_grad: float32 [16384], P(('dp', 'shard')), may hold values from -6 to 6
Outputs:
- logits: float32 [16384], P(('dp', 'shard'))
- grad_cross: float32 [1024, 1024], replicated
- grad_top: float32 [1024, 512], replicated
- grad_cross_bias: float32 [1024], replicated
- grad_top_bias: float32 [512], replicated
- grad_out: float32 [512], replicated
- table_grad: float32 [16384, 128], P('shard')
The draws below stay inside these ranges and needn't reach their ends.
Inputs may be any that keep to these rules, and one draw needn't show every extreme that they name: `wanted`: the 128 rows that one device fetches from one owner are distinct.
All inputs are finite; a program needn't handle non-finite values.
Results may differ from the reference program's by a relative error of at most 0.0084.
Values sent between devices are 32-bit elements; how exact they have to be, the bound alone decides.
No kernel may reach another device: no remote copies, remote signals or barrier semaphores. Data moves between devices by JAX's collectives and lax.ppermute only.
A program may use at most 128 MiB of HBM per device.

```python
import jax
import jax.numpy as jnp
from jax import lax

D_EMB = 128
FEATS = 8
TOP = 512
BAG = 4
ROWS_DEV = 2048
CAP = 128
SAMPLES_DEV = 512
WIDTH = 1024
TABLE_ROWS = 16384
SAMPLES = 16384
N_SHARD = 8
DEVICES = 32


def draw_wanted(key, part):
    order_keys = jax.random.split(jax.random.fold_in(key, 11), N_SHARD)
    ranking = jax.vmap(lambda one: jax.random.permutation(one, ROWS_DEV))(order_keys).astype(jnp.int32)
    divisor = ranking // 8 + 1
    raw_scores = jax.random.randint(jax.random.fold_in(key, 12), (DEVICES, N_SHARD, ROWS_DEV), 0, 65536, dtype=jnp.int32)
    scores = raw_scores // divisor[None] * ROWS_DEV + jnp.arange(ROWS_DEV, dtype=jnp.int32)[None, None, :]
    unused, picked = lax.top_k(scores, CAP)
    return picked.astype(jnp.int32)


def place_ends(result, stream_key, smallest, largest):
    index_at = [jax.random.randint(jax.random.fold_in(stream_key, axis), (), 0, length) for axis, length in enumerate(result.shape)]
    widest = result.shape.index(max(result.shape))
    neighbour = index_at[:widest] + [(index_at[widest] + 1) % result.shape[widest]] + index_at[widest + 1:]
    return result.at[tuple(index_at)].set(smallest).at[tuple(neighbour)].set(largest)


def block_scale(stream_key, extent, cuts, low, largest):
    level = 1.0
    for dim, shards_of in cuts:
        draws = jax.random.uniform(jax.random.fold_in(jax.random.fold_in(stream_key, 6), dim), (shards_of,), jnp.float32, low / len(cuts), largest / len(cuts))
        level = level * jnp.repeat(jnp.exp(draws), extent[dim] // shards_of).reshape((-1,) + (1,) * (len(extent) - 1 - dim))
    return level


def bell_draw(own_key, extent, deviation, reach, cuts=(), held_as=jnp.bfloat16):
    loudness = block_scale(own_key, extent, cuts, -0.22, 0.18) if cuts else 1.0
    drawn = jax.random.normal(own_key, extent, jnp.float32) * deviation * loudness
    return jnp.minimum(jnp.maximum(drawn, -reach), reach).astype(held_as)


def setup_inputs(seed: int = 0) -> dict:
    streams_of = jax.random.split(jax.random.key(seed), 11)
    return {
        "table": bell_draw(streams_of[0], (TABLE_ROWS, D_EMB), 1.0, 6.0, ((0, 8),), jnp.float32),
        "cross_weight": bell_draw(streams_of[1], (WIDTH, WIDTH), WIDTH ** -0.5, 0.1875),
        "cross_bias": bell_draw(streams_of[2], (WIDTH,), 0.5, 3.0, (), jnp.float32),
        "top_weight": bell_draw(streams_of[3], (WIDTH, TOP), WIDTH ** -0.5, 0.1875),
        "top_bias": bell_draw(streams_of[4], (TOP,), 0.5, 3.0, (), jnp.float32),
        "out_weight": bell_draw(streams_of[5], (TOP,), TOP ** -0.5, 0.25, (), jnp.float32),
        "wanted": draw_wanted(jax.random.fold_in(streams_of[10], 71), 0),
        "slots": place_ends(jax.random.randint(streams_of[7], (SAMPLES, FEATS, BAG), 0, N_SHARD * CAP), jax.random.fold_in(streams_of[7], 1), 0, (N_SHARD * CAP) - 1).astype(jnp.int32),
        "lengths": place_ends(jax.random.randint(streams_of[8], (SAMPLES, FEATS), 1, BAG + 1), jax.random.fold_in(streams_of[8], 1), 1, BAG).astype(jnp.int32),
        "logit_grad": bell_draw(streams_of[9], (SAMPLES,), 1.0, 6.0, ((0, 32),), jnp.float32),
    }


def reference(table, cross_weight, cross_bias, top_weight, top_bias, out_weight, wanted, slots, lengths, logit_grad):
    owners = (jnp.arange(N_SHARD, dtype=jnp.int32) * ROWS_DEV)[:, None]
    devices = wanted.shape[0]
    slot_dev = slots.reshape(devices, SAMPLES_DEV, FEATS, BAG)
    len_dev = lengths.reshape(devices, SAMPLES_DEV, FEATS)
    grad_dev = logit_grad.reshape(devices, SAMPLES_DEV)

    def device_step(carry, inputs):
        g_cross, g_top, g_cbias, g_tbias, g_out, t_grad = carry
        want_here, slot_here, len_here, cot = inputs
        rowmap = (owners + want_here).reshape(-1).astype(jnp.int32)
        row_ids = rowmap[slot_here]
        live = (jnp.arange(BAG, dtype=jnp.int32)[None, None, :] < len_here[:, :, None]).astype(jnp.float32)
        gathered = table[row_ids]
        pooled = jnp.sum(gathered * live[..., None], axis=2)
        x0 = pooled.reshape(SAMPLES_DEV, FEATS * D_EMB).astype(jnp.bfloat16)
        xfull = x0.astype(jnp.float32)
        yval = jnp.dot(x0, cross_weight, preferred_element_type=jnp.float32) + cross_bias
        hidden = (xfull * yval + xfull).astype(jnp.bfloat16)
        zval = jnp.dot(hidden, top_weight, preferred_element_type=jnp.float32) + top_bias
        sig = jax.nn.sigmoid(zval)
        uval = zval * sig
        logit = jnp.dot(uval, out_weight, precision=lax.Precision.HIGHEST)
        g_out = g_out + jnp.dot(cot, uval, precision=lax.Precision.HIGHEST)
        dz = cot[:, None] * out_weight[None, :] * (sig * (1.0 + zval * (1.0 - sig)))
        dzb = dz.astype(jnp.bfloat16)
        g_top = g_top + jnp.dot(hidden.T, dzb, preferred_element_type=jnp.float32)
        g_tbias = g_tbias + jnp.sum(dz, axis=0)
        dh = jnp.dot(dzb, top_weight.T, preferred_element_type=jnp.float32)
        dy = dh * xfull
        dyb = dy.astype(jnp.bfloat16)
        g_cross = g_cross + jnp.dot(x0.T, dyb, preferred_element_type=jnp.float32)
        g_cbias = g_cbias + jnp.sum(dy, axis=0)
        dx = dh * (yval + 1.0) + jnp.dot(dyb, cross_weight.T, preferred_element_type=jnp.float32)
        contrib = dx.reshape(SAMPLES_DEV, FEATS, 1, D_EMB) * live[..., None]
        t_grad = t_grad.at[row_ids.reshape(-1)].add(contrib.reshape(-1, D_EMB))
        return (g_cross, g_top, g_cbias, g_tbias, g_out, t_grad), logit

    width = FEATS * D_EMB
    init = (jnp.zeros((width, width), jnp.float32), jnp.zeros((width, TOP), jnp.float32),
            jnp.zeros((width,), jnp.float32), jnp.zeros((TOP,), jnp.float32),
            jnp.zeros((TOP,), jnp.float32), jnp.zeros(table.shape, jnp.float32))
    final, logit_all = lax.scan(device_step, init, (wanted, slot_dev, len_dev, grad_dev))
    g_cross, g_top, g_cbias, g_tbias, g_out, t_grad = final
    return (logit_all.reshape(-1), g_cross, g_top, g_cbias, g_tbias, g_out, t_grad)
```

```python
import functools

import jax
import jax.numpy as jnp
from jax import lax
from jax.experimental import pallas as pl
from jax.experimental.pallas import tpu as pltpu
from jax.sharding import PartitionSpec as P


F32 = jnp.float32
BF16 = jnp.bfloat16
MIB = 1 << 20
NN = (((1,), (0,)), ((), ()))
NT = (((1,), (1,)), ((), ()))


def dot(a, b, dims=NN):
    return lax.dot_general(a, b, dims, preferred_element_type=F32)


def split(v):
    hi = v.astype(BF16)
    return hi, (v - hi.astype(F32)).astype(BF16)


def params(limit, semantics=None):
    return pltpu.CompilerParams(vmem_limit_bytes=limit, dimension_semantics=semantics)


def cost(flops, bytes_accessed):
    return pl.CostEstimate(flops=flops, bytes_accessed=bytes_accessed, transcendentals=0)


def gather_kernel(ids_ref, table_ref, out_ref):
    step = 16

    def body(i, carry):
        for j in range(step):
            at = i * step + j
            out_ref[pl.ds(at, 1), :] = table_ref[pl.ds(ids_ref[at], 1), :]
        return carry

    lax.fori_loop(0, out_ref.shape[0] // step, body, 0)


def gather_rows(table, ids):
    n, emb = ids.shape[0], table.shape[1]
    return pl.pallas_call(
        gather_kernel,
        out_shape=jax.ShapeDtypeStruct((n, emb), F32),
        grid_spec=pltpu.PrefetchScalarGridSpec(
            num_scalar_prefetch=1,
            grid=(1,),
            in_specs=[pl.BlockSpec(table.shape, lambda i, ids: (0, 0))],
            out_specs=pl.BlockSpec((n, emb), lambda i, ids: (0, 0)),
        ),
        compiler_params=params(16 * MIB),
        cost_estimate=cost(0, 8 * n * emb),
        name="gather_rows",
    )(ids, table)


def hot_kernel(slots_ref, len_ref, hot_ref):
    f = pl.program_id(0)
    bag, samples = slots_ref.shape[1], slots_ref.shape[2]
    count = len_ref[pl.ds(f, 1), :]
    keys = [jnp.where(b < count, slots_ref[0, b : b + 1, :], -1) for b in range(bag)]
    chunk = 32

    def body(i, carry):
        base = pl.multiple_of(i * chunk, chunk)
        place = lax.broadcasted_iota(jnp.int32, (chunk, samples), 0) + base
        total = jnp.zeros((chunk, samples), F32)
        for key in keys:
            total = total + jnp.where(place == key, 1.0, 0.0)
        hot_ref[0, pl.ds(base, chunk), :] = total.astype(BF16)
        return carry

    lax.fori_loop(0, hot_ref.shape[1] // chunk, body, 0)


def multi_hot(slots_t, lengths_t, places):
    feats, bag, samples = slots_t.shape
    return pl.pallas_call(
        hot_kernel,
        out_shape=jax.ShapeDtypeStruct((feats, places, samples), BF16),
        grid=(feats,),
        in_specs=[
            pl.BlockSpec((1, bag, samples), lambda f: (f, 0, 0)),
            pl.BlockSpec((feats, samples), lambda f: (0, 0)),
        ],
        out_specs=pl.BlockSpec((1, places, samples), lambda f: (f, 0, 0)),
        compiler_params=params(32 * MIB),
        cost_estimate=cost(feats * places * samples * 8, feats * places * samples * 2),
        name="multi_hot",
    )(slots_t, lengths_t)


def dense_kernel(
    code_ref, rows_ref, hot_ref, cwt_ref, twt_ref, tw_ref, cb_ref, tb_ref, ow_ref, lg_ref,
    logits_ref, small_ref, dyb_ref, dxa_ref, ka_ref, sa_ref, kb_ref, sb_ref, kc_ref, sc_ref,
    rt_ref, x0_ref, y_ref, h_ref, dz_ref, perm_ref,
    *, blocks,
):
    f = pl.program_id(0)
    emb = rows_ref.shape[1]
    width, samples = x0_ref.shape
    top = dz_ref.shape[0]
    tile = 256

    @pl.when(f == 0)
    def _():
        hi, lo = split(rows_ref[...].T)
        rt_ref[:emb, :] = hi
        rt_ref[emb:, :] = lo

    both = dot(rt_ref[...], hot_ref[0])
    x0_ref[pl.ds(pl.multiple_of(f * emb, emb), emb), :] = (both[:emb] + both[emb:]).astype(BF16)

    @pl.when(f == pl.num_programs(0) - 1)
    def _():
        ones = jnp.ones((8, 128), BF16)

        def row_sums(v, at):
            part = v[:, :128]
            for k in range(128, samples, 128):
                part = part + v[:, k : k + 128]
            hi, lo = split(part)
            total = dot(ones, hi, NT) + dot(ones, lo, NT)
            small_ref[:, at : at + v.shape[0]] = total[0:1]

        def relative(src_ref, code):
            n = width // blocks
            for r in range(blocks):
                at = pl.multiple_of((code ^ r) * n, n)
                perm_ref[r * n : (r + 1) * n, :] = src_ref[pl.ds(at, n), :]

        def gradient(keep_ref, send_ref, right):
            half = width // 2
            for i in range(0, half, tile):
                send_ref[i : i + tile, :] = dot(perm_ref[half + i : half + i + tile, :], right, NT)
            for i in range(0, half, tile):
                keep_ref[i : i + tile, :] = dot(perm_ref[i : i + tile, :], right, NT)

        for i in range(0, width, tile):
            y = dot(cwt_ref[i : i + tile, :], x0_ref[...]) + cb_ref[i : i + tile, :]
            x = x0_ref[i : i + tile, :].astype(F32)
            y_ref[i : i + tile, :] = y
            h_ref[i : i + tile, :] = (x * y + x).astype(BF16)
        lg = lg_ref[...]
        logits = jnp.zeros((1, samples), F32)
        for i in range(0, top, tile):
            z = dot(twt_ref[i : i + tile, :], h_ref[...]) + tb_ref[i : i + tile, :]
            ow = ow_ref[i : i + tile, :]
            g = jax.nn.sigmoid(z)
            u = z * g
            logits = logits + jnp.sum(u * ow, axis=0, keepdims=True)
            dz = ow * lg * (g * (1.0 + z * (1.0 - g)))
            dz_ref[i : i + tile, :] = dz.astype(BF16)
            row_sums(dz, width + i)
            row_sums(lg * u, width + top + i)
        logits_ref[...] = logits
        relative(h_ref, code_ref[2])
        gradient(kc_ref, sc_ref, dz_ref[...])
        for i in range(0, width, tile):
            dh = dot(tw_ref[i : i + tile, :], dz_ref[...])
            dy = dh * x0_ref[i : i + tile, :].astype(F32)
            dyb_ref[i : i + tile, :] = dy.astype(BF16)
            dxa_ref[i : i + tile, :] = dh * (y_ref[i : i + tile, :] + 1.0)
            row_sums(dy, i)
        relative(x0_ref, code_ref[0])
        gradient(ka_ref, sa_ref, dyb_ref[: width // 2, :])
        relative(x0_ref, code_ref[1])
        gradient(kb_ref, sb_ref, dyb_ref[width // 2 :, :])


def dense(codes, rows, hot, cwt, twt, tw, cb, tb, ow, lg, blocks):
    feats, places, samples = hot.shape
    emb = rows.shape[1]
    width, top = tw.shape
    half = width // 2

    def whole(shape):
        return pl.BlockSpec(shape, lambda f, c: (0, 0))

    outs = [(1, samples), (1, width + 2 * top)]
    out_shape = [jax.ShapeDtypeStruct(s, F32) for s in outs]
    out_shape += [jax.ShapeDtypeStruct((width, samples), BF16)]
    out_shape += [jax.ShapeDtypeStruct((width, samples), F32)]
    out_shape += [jax.ShapeDtypeStruct((half, half), F32)] * 4
    out_shape += [jax.ShapeDtypeStruct((half, top), F32)] * 2
    return pl.pallas_call(
        functools.partial(dense_kernel, blocks=blocks),
        out_shape=out_shape,
        grid_spec=pltpu.PrefetchScalarGridSpec(
            num_scalar_prefetch=1,
            grid=(feats,),
            in_specs=[
                whole(rows.shape),
                pl.BlockSpec((1, places, samples), lambda f, c: (f, 0, 0)),
                *[whole(v.shape) for v in (cwt, twt, tw, cb, tb, ow, lg)],
            ],
            out_specs=[whole(s.shape) for s in out_shape],
            scratch_shapes=[
                pltpu.VMEM((2 * emb, places), BF16),
                pltpu.VMEM((width, samples), BF16),
                pltpu.VMEM((width, samples), F32),
                pltpu.VMEM((width, samples), BF16),
                pltpu.VMEM((top, samples), BF16),
                pltpu.VMEM((width, samples), BF16),
            ],
        ),
        compiler_params=params(60 * MIB, ("arbitrary",)),
        cost_estimate=cost(10**10, 24 * MIB),
        name="dense",
    )(codes, rows, hot, cwt, twt, tw, cb, tb, ow, lg)


def slot_kernel(dxa_ref, cw_ref, dyb_ref, hot_ref, out_ref, total_ref):
    f = pl.program_id(0)
    emb = out_ref.shape[1]
    dx = dxa_ref[...] + dot(cw_ref[...], dyb_ref[...])
    pair = jnp.concatenate(split(dx), axis=0)
    term = dot(hot_ref[0], pair, NT)

    @pl.when(f == 0)
    def _():
        total_ref[...] = term

    @pl.when(f > 0)
    def _():
        total_ref[...] += term

    @pl.when(f == pl.num_programs(0) - 1)
    def _():
        out_ref[...] = total_ref[:, :emb] + total_ref[:, emb:]


def slot_gradients(dxa, cw, dyb, hot):
    feats, places, samples = hot.shape
    width = cw.shape[0]
    emb = width // feats
    return pl.pallas_call(
        slot_kernel,
        out_shape=jax.ShapeDtypeStruct((places, emb), F32),
        grid=(feats,),
        in_specs=[
            pl.BlockSpec((emb, samples), lambda f: (f, 0)),
            pl.BlockSpec((emb, width), lambda f: (f, 0)),
            pl.BlockSpec((width, samples), lambda f: (0, 0)),
            pl.BlockSpec((1, places, samples), lambda f: (f, 0, 0)),
        ],
        out_specs=pl.BlockSpec((places, emb), lambda f: (0, 0)),
        scratch_shapes=[pltpu.VMEM((places, 2 * emb), F32)],
        compiler_params=params(40 * MIB, ("arbitrary",)),
        cost_estimate=cost(4 * 10**9, 16 * MIB),
        name="slot_gradients",
    )(dxa, cw, dyb, hot)


def table_kernel(code_ref, ids_ref, grads_ref, keep_ref, send_ref, pair_ref):
    n, emb = grads_ref.shape
    half = keep_ref.shape[0]
    hi, lo = split(grads_ref[...])
    pair_ref[:, :emb] = hi
    pair_ref[:, emb:] = lo
    tile = 256
    for part, out_ref in ((1, send_ref), (0, keep_ref)):
        base = (code_ref[0] ^ part) * half
        for i in range(0, half, tile):
            place = lax.broadcasted_iota(jnp.int32, (tile, n), 0) + (base + i)
            hot = jnp.where(place == ids_ref[...], 1.0, 0.0).astype(BF16)
            both = dot(hot, pair_ref[...])
            out_ref[i : i + tile, :] = both[:, :emb] + both[:, emb:]


def table_sums(core, ids, grads, rows):
    n, emb = grads.shape
    half = rows // 2

    def whole(shape):
        return pl.BlockSpec(shape, lambda i, c: (0, 0))

    return pl.pallas_call(
        table_kernel,
        out_shape=[jax.ShapeDtypeStruct((half, emb), F32)] * 2,
        grid_spec=pltpu.PrefetchScalarGridSpec(
            num_scalar_prefetch=1,
            grid=(1,),
            in_specs=[whole((1, n)), whole((n, emb))],
            out_specs=[whole((half, emb))] * 2,
            scratch_shapes=[pltpu.VMEM((n, 2 * emb), BF16)],
        ),
        compiler_params=params(40 * MIB),
        cost_estimate=cost(2 * 10**9, 2 * MIB),
        name="table_sums",
    )(core, ids, grads)


def place_kernel(code_ref, a_ref, b_ref, c_ref, cross_ref, top_ref, *, blocks):
    width, half = a_ref.shape
    n = width // blocks
    for r in range(blocks):
        rows = slice(r * n, (r + 1) * n)
        at = [pl.ds(pl.multiple_of((code_ref[k] ^ r) * n, n), n) for k in range(3)]
        cross_ref[at[0], :half] = a_ref[rows, :]
        cross_ref[at[1], half:] = b_ref[rows, :]
        top_ref[at[2], :] = c_ref[rows, :]


def place(codes, a, b, c, blocks):
    width, half = a.shape

    def whole(shape):
        return pl.BlockSpec(shape, lambda i, k: (0, 0))

    return pl.pallas_call(
        functools.partial(place_kernel, blocks=blocks),
        out_shape=[
            jax.ShapeDtypeStruct((width, 2 * half), F32),
            jax.ShapeDtypeStruct(c.shape, F32),
        ],
        grid_spec=pltpu.PrefetchScalarGridSpec(
            num_scalar_prefetch=1,
            grid=(1,),
            in_specs=[whole(v.shape) for v in (a, b, c)],
            out_specs=[whole((width, 2 * half)), whole(c.shape)],
        ),
        compiler_params=params(40 * MIB),
        name="place",
    )(codes, a, b, c)


def on_device(
    sizes,
    table,
    cross_weight,
    cross_bias,
    top_weight,
    top_bias,
    out_weight,
    wanted,
    slots,
    lengths,
    logit_grad,
):
    emb = table.shape[1]
    width, top = top_weight.shape
    n_dp, n_shard = sizes["dp"].bit_length() - 1, sizes["shard"].bit_length() - 1
    n_y = n_shard // 2
    core = [("dp", 0)]
    along_x = [("dp", k) for k in range(1, n_dp)]
    along_y = [("shard", k) for k in range(n_y)]
    along_z = [("shard", k) for k in range(n_y, n_shard)]
    colours = [
        core + along_x + along_y + along_z,
        core + along_y + along_x + along_z,
        core + along_z + along_x + along_y,
    ]
    smallest = 16
    depth = min(n_dp + n_shard, (width // smallest).bit_length() - 1)
    blocks = 1 << depth
    position = {axis: lax.axis_index(axis) for axis in sizes}

    def bit(step):
        return (position[step[0]] >> step[1]) & 1

    def code(steps):
        total = jnp.int32(0)
        for step in steps[:depth]:
            total = total * 2 + bit(step)
        return total.astype(jnp.int32)

    def swap(v, step):
        axis, k = step
        return lax.ppermute(v, axis, [(i, i ^ (1 << k)) for i in range(sizes[axis])])

    codes = jnp.stack([code(c) for c in colours])
    my_core = bit(core[0]).astype(jnp.int32).reshape(1)

    requests = wanted[0]
    served = lax.all_to_all(requests, "shard", split_axis=0, concat_axis=0, tiled=True)
    ids = served.reshape(-1)
    sent = gather_rows(table, ids).reshape(requests.shape + (emb,))
    cache = lax.all_to_all(sent, "shard", split_axis=0, concat_axis=0, tiled=True)
    rows = cache.reshape(-1, emb)

    hot = multi_hot(slots.transpose(1, 2, 0), lengths.T, rows.shape[0])
    logits, small, dyb, dxa, ka, sa, kb, sb, kc, sc = dense(
        codes, rows, hot, cross_weight.T, top_weight.T, top_weight,
        cross_bias[:, None], top_bias[:, None], out_weight[:, None], logit_grad[None, :], blocks,
    )
    steps = len(colours[0])
    state = [[ka, sa], [kb, sb], [kc, sc]]
    for t in range(steps):
        got = [swap(s[1] if t < depth else s[0], c[t]) for s, c in zip(state, colours)]
        small = small + swap(small, colours[0][t])
        for s, g in zip(state, got):
            total = s[0] + g
            if t + 1 < depth:
                h = total.shape[0] // 2
                s[:] = [total[:h], total[h:]]
            else:
                s[:] = [total, None]
        if t + 1 < steps:
            keep = [v for s in state for v in s if v is not None] + [small]
            keep = list(lax.optimization_barrier(tuple(keep)))
            small = keep.pop()
            for s in state:
                s[:] = [keep.pop(0), keep.pop(0) if s[1] is not None else None]
    full = [s[0] for s in state]
    for t in reversed(range(depth)):
        got = [swap(v, c[t]) for v, c in zip(full, colours)]
        full = [jnp.concatenate([v, g]) for v, g in zip(full, got)]
        if t:
            full = list(lax.optimization_barrier(tuple(full)))
    g_cross, g_top = place(codes, *full, blocks)

    slot_grads = slot_gradients(dxa, cross_weight, dyb, hot).reshape(cache.shape)
    returned = lax.all_to_all(slot_grads, "shard", split_axis=0, concat_axis=0, tiled=True)
    keep, send = table_sums(my_core, ids[None, :], returned.reshape(-1, emb), table.shape[0])
    part = keep + swap(send, core[0])
    for step in along_x:
        part = part + swap(part, step)
    other = swap(part, core[0])
    first = my_core[0] == 0
    table_grad = jnp.concatenate([jnp.where(first, part, other), jnp.where(first, other, part)])
    small = small[0]
    return (
        logits[0], g_cross, g_top, small[:width], small[width : width + top],
        small[width + top :], table_grad,
    )


def solution(mesh):
    placed = (
        P("shard", None),
        P(),
        P(),
        P(),
        P(),
        P(),
        P(("dp", "shard"), None, None),
        P(("dp", "shard"), None, None),
        P(("dp", "shard"), None),
        P(("dp", "shard")),
    )
    return jax.shard_map(
        functools.partial(on_device, dict(mesh.shape)),
        mesh=mesh,
        in_specs=placed,
        out_specs=(P(("dp", "shard")), P(), P(), P(), P(), P(), P("shard", None)),
        check_vma=False,
    )
```

```python
import functools

import jax
import jax.numpy as jnp
from jax import lax
from jax.experimental import pallas as pl
from jax.experimental.pallas import tpu as pltpu
from jax.sharding import PartitionSpec as P


F32 = jnp.float32
BF16 = jnp.bfloat16
MIB = 1 << 20
FORWARD_LIMIT = 30 * MIB
BACKWARD_LIMIT = 30 * MIB
PLACE_LIMIT = 16 * MIB
NN = (((1,), (0,)), ((), ()))
NT = (((1,), (1,)), ((), ()))


def dot(a, b, dims=NN):
    return lax.dot_general(a, b, dims, preferred_element_type=F32)


def split(v):
    hi = v.astype(BF16)
    return hi, (v - hi.astype(F32)).astype(BF16)


def params(limit, semantics=None):
    return pltpu.CompilerParams(vmem_limit_bytes=limit, dimension_semantics=semantics)


def cost(flops, bytes_accessed):
    return pl.CostEstimate(flops=flops, bytes_accessed=bytes_accessed, transcendentals=0)


def gather_kernel(ids_ref, table_ref, out_ref):
    step = 16

    def body(i, carry):
        for j in range(step):
            at = i * step + j
            out_ref[pl.ds(at, 1), :] = table_ref[pl.ds(ids_ref[at], 1), :]
        return carry

    lax.fori_loop(0, out_ref.shape[0] // step, body, 0)


def gather_rows(table, ids):
    n, emb = ids.shape[0], table.shape[1]
    return pl.pallas_call(
        gather_kernel,
        out_shape=jax.ShapeDtypeStruct((n, emb), F32),
        grid_spec=pltpu.PrefetchScalarGridSpec(
            num_scalar_prefetch=1,
            grid=(1,),
            in_specs=[pl.BlockSpec(table.shape, lambda i, ids: (0, 0))],
            out_specs=pl.BlockSpec((n, emb), lambda i, ids: (0, 0)),
        ),
        compiler_params=params(16 * MIB),
        cost_estimate=cost(0, 8 * n * emb),
        name="gather_rows",
    )(ids, table)


def hot_kernel(slots_ref, len_ref, hot_ref):
    f = pl.program_id(0)
    bag, samples = slots_ref.shape[1], slots_ref.shape[2]
    count = len_ref[pl.ds(f, 1), :]
    keys = [jnp.where(b < count, slots_ref[0, b : b + 1, :], -1) for b in range(bag)]
    chunk = 32

    def body(i, carry):
        base = pl.multiple_of(i * chunk, chunk)
        place = lax.broadcasted_iota(jnp.int32, (chunk, samples), 0) + base
        total = jnp.zeros((chunk, samples), F32)
        for key in keys:
            total = total + jnp.where(place == key, 1.0, 0.0)
        hot_ref[0, pl.ds(base, chunk), :] = total.astype(BF16)
        return carry

    lax.fori_loop(0, hot_ref.shape[1] // chunk, body, 0)


def multi_hot(slots_t, lengths_t, places):
    feats, bag, samples = slots_t.shape
    return pl.pallas_call(
        hot_kernel,
        out_shape=jax.ShapeDtypeStruct((feats, places, samples), BF16),
        grid=(feats,),
        in_specs=[
            pl.BlockSpec((1, bag, samples), lambda f: (f, 0, 0)),
            pl.BlockSpec((feats, samples), lambda f: (0, 0)),
        ],
        out_specs=pl.BlockSpec((1, places, samples), lambda f: (f, 0, 0)),
        compiler_params=params(32 * MIB),
        cost_estimate=cost(feats * places * samples * 8, feats * places * samples * 2),
        name="multi_hot",
    )(slots_t, lengths_t)


def row_sums(v):
    samples = v.shape[1]
    part = v[:, :128]
    for k in range(128, samples, 128):
        part = part + v[:, k : k + 128]
    hi, lo = split(part)
    ones = jnp.ones((8, 128), BF16)
    return (dot(ones, hi, NT) + dot(ones, lo, NT))[0:1]


def relative(dst_ref, src_ref, code, blocks):
    n = src_ref.shape[0] // blocks
    for r in range(blocks):
        at = pl.multiple_of((code ^ r) * n, n)
        dst_ref[r * n : (r + 1) * n, :] = src_ref[pl.ds(at, n), :]


def forward_kernel(
    code_ref, rows_ref, hot_ref, cwt_any, twt_any, cb_ref, tb_ref, ow_ref, lg_ref,
    logits_ref, small_ref, x0_ref, y_ref, dz_ref, kc_ref, sc_ref,
    rt_ref, h_ref, perm_ref, cwt_ref, twt_ref, sem,
    *, blocks,
):
    f = pl.program_id(0)
    emb = rows_ref.shape[1]
    width, samples = x0_ref.shape
    top = dz_ref.shape[0]
    tile = 256
    loads = [
        pltpu.make_async_copy(cwt_any, cwt_ref, sem.at[0]),
        pltpu.make_async_copy(twt_any, twt_ref, sem.at[1]),
    ]

    @pl.when(f == 0)
    def _():
        for load in loads:
            load.start()
        hi, lo = split(rows_ref[...].T)
        rt_ref[:emb, :] = hi
        rt_ref[emb:, :] = lo

    both = dot(rt_ref[...], hot_ref[0])
    x0_ref[pl.ds(pl.multiple_of(f * emb, emb), emb), :] = (both[:emb] + both[emb:]).astype(BF16)

    @pl.when(f == pl.num_programs(0) - 1)
    def _():
        loads[0].wait()
        for i in range(0, width, tile):
            y = dot(cwt_ref[i : i + tile, :], x0_ref[...]) + cb_ref[i : i + tile, :]
            x = x0_ref[i : i + tile, :].astype(F32)
            y_ref[i : i + tile, :] = y
            h_ref[i : i + tile, :] = (x * y + x).astype(BF16)
        loads[1].wait()
        lg = lg_ref[...]
        logits = jnp.zeros((1, samples), F32)
        for i in range(0, top, tile):
            z = dot(twt_ref[i : i + tile, :], h_ref[...]) + tb_ref[i : i + tile, :]
            ow = ow_ref[i : i + tile, :]
            g = jax.nn.sigmoid(z)
            u = z * g
            logits = logits + jnp.sum(u * ow, axis=0, keepdims=True)
            dz = ow * lg * (g * (1.0 + z * (1.0 - g)))
            dz_ref[i : i + tile, :] = dz.astype(BF16)
            small_ref[:, i : i + tile] = row_sums(dz)
            small_ref[:, top + i : top + i + tile] = row_sums(lg * u)
        logits_ref[...] = logits
        relative(perm_ref, h_ref, code_ref[2], blocks)
        half = width // 2
        sc_ref[...] = dot(perm_ref[half:, :], dz_ref[...], NT)
        kc_ref[...] = dot(perm_ref[:half, :], dz_ref[...], NT)


def forward(codes, rows, hot, cwt, twt, cb, tb, ow, lg, blocks):
    feats, places, samples = hot.shape
    emb = rows.shape[1]
    top, width = twt.shape
    half = width // 2

    def whole(shape):
        return pl.BlockSpec(shape, lambda f, c: (0, 0))

    out_shape = [
        jax.ShapeDtypeStruct((1, samples), F32),
        jax.ShapeDtypeStruct((1, 2 * top), F32),
        jax.ShapeDtypeStruct((width, samples), BF16),
        jax.ShapeDtypeStruct((width, samples), F32),
        jax.ShapeDtypeStruct((top, samples), BF16),
        jax.ShapeDtypeStruct((half, top), F32),
        jax.ShapeDtypeStruct((half, top), F32),
    ]
    return pl.pallas_call(
        functools.partial(forward_kernel, blocks=blocks),
        out_shape=out_shape,
        grid_spec=pltpu.PrefetchScalarGridSpec(
            num_scalar_prefetch=1,
            grid=(feats,),
            in_specs=[
                whole(rows.shape),
                pl.BlockSpec((1, places, samples), lambda f, c: (f, 0, 0)),
                pl.BlockSpec(memory_space=pl.ANY),
                pl.BlockSpec(memory_space=pl.ANY),
                *[whole(v.shape) for v in (cb, tb, ow, lg)],
            ],
            out_specs=[whole(s.shape) for s in out_shape],
            scratch_shapes=[
                pltpu.VMEM((2 * emb, places), BF16),
                pltpu.VMEM((width, samples), BF16),
                pltpu.VMEM((width, samples), BF16),
                pltpu.VMEM((width, width), BF16),
                pltpu.VMEM((top, width), BF16),
                pltpu.SemaphoreType.DMA((2,)),
            ],
        ),
        compiler_params=params(FORWARD_LIMIT, ("arbitrary",)),
        cost_estimate=cost(6 * 10**9, 16 * MIB),
        name="forward",
    )(codes, rows, hot, cwt, twt, cb, tb, ow, lg)


def backward_kernel(
    code_ref, x0_ref, y_ref, dz_ref, tw_ref,
    small_ref, dyb_ref, dxa_ref, ka_ref, sa_ref, kb_ref, sb_ref,
    perm_ref, *, blocks,
):
    width = x0_ref.shape[0]
    half = width // 2
    tile = 256

    def upper(low):
        for i in range(low, low + half, tile):
            dh = dot(tw_ref[i : i + tile, :], dz_ref[...])
            dy = dh * x0_ref[i : i + tile, :].astype(F32)
            dyb_ref[i : i + tile, :] = dy.astype(BF16)
            dxa_ref[i : i + tile, :] = dh * (y_ref[i : i + tile, :] + 1.0)
            small_ref[:, i : i + tile] = row_sums(dy)

    for k, (keep_ref, send_ref) in enumerate(((ka_ref, sa_ref), (kb_ref, sb_ref))):
        upper(k * half)
        relative(perm_ref, x0_ref, code_ref[k], blocks)
        right = dyb_ref[k * half : (k + 1) * half, :]
        send_ref[...] = dot(perm_ref[half:, :], right, NT)
        keep_ref[...] = dot(perm_ref[:half, :], right, NT)


def backward(codes, x0, y, dz, tw, blocks):
    width, samples = x0.shape
    half = width // 2

    def whole(shape):
        return pl.BlockSpec(shape, lambda f, c: (0, 0))

    out_shape = [
        jax.ShapeDtypeStruct((1, width), F32),
        jax.ShapeDtypeStruct((width, samples), BF16),
        jax.ShapeDtypeStruct((width, samples), F32),
    ] + [jax.ShapeDtypeStruct((half, half), F32)] * 4
    return pl.pallas_call(
        functools.partial(backward_kernel, blocks=blocks),
        out_shape=out_shape,
        grid_spec=pltpu.PrefetchScalarGridSpec(
            num_scalar_prefetch=1,
            grid=(1,),
            in_specs=[whole(v.shape) for v in (x0, y, dz, tw)],
            out_specs=[whole(s.shape) for s in out_shape],
            scratch_shapes=[pltpu.VMEM((width, samples), BF16)],
        ),
        compiler_params=params(BACKWARD_LIMIT, ("arbitrary",)),
        cost_estimate=cost(4 * 10**9, 12 * MIB),
        name="backward",
    )(codes, x0, y, dz, tw)


def slot_kernel(dxa_ref, cw_ref, dyb_ref, hot_ref, out_ref, total_ref):
    f = pl.program_id(0)
    emb = out_ref.shape[1]
    dx = dxa_ref[...] + dot(cw_ref[...], dyb_ref[...])
    pair = jnp.concatenate(split(dx), axis=0)
    term = dot(hot_ref[0], pair, NT)

    @pl.when(f == 0)
    def _():
        total_ref[...] = term

    @pl.when(f > 0)
    def _():
        total_ref[...] += term

    @pl.when(f == pl.num_programs(0) - 1)
    def _():
        out_ref[...] = total_ref[:, :emb] + total_ref[:, emb:]


def slot_gradients(dxa, cw, dyb, hot):
    feats, places, samples = hot.shape
    width = cw.shape[0]
    emb = width // feats
    return pl.pallas_call(
        slot_kernel,
        out_shape=jax.ShapeDtypeStruct((places, emb), F32),
        grid=(feats,),
        in_specs=[
            pl.BlockSpec((emb, samples), lambda f: (f, 0)),
            pl.BlockSpec((emb, width), lambda f: (f, 0)),
            pl.BlockSpec((width, samples), lambda f: (0, 0)),
            pl.BlockSpec((1, places, samples), lambda f: (f, 0, 0)),
        ],
        out_specs=pl.BlockSpec((places, emb), lambda f: (0, 0)),
        scratch_shapes=[pltpu.VMEM((places, 2 * emb), F32)],
        compiler_params=params(40 * MIB, ("arbitrary",)),
        cost_estimate=cost(4 * 10**9, 16 * MIB),
        name="slot_gradients",
    )(dxa, cw, dyb, hot)


def table_kernel(code_ref, ids_ref, grads_ref, keep_ref, send_ref, pair_ref):
    n, emb = grads_ref.shape
    half = keep_ref.shape[0]
    hi, lo = split(grads_ref[...])
    pair_ref[:, :emb] = hi
    pair_ref[:, emb:] = lo
    tile = 256
    for part, out_ref in ((1, send_ref), (0, keep_ref)):
        base = (code_ref[0] ^ part) * half
        for i in range(0, half, tile):
            place = lax.broadcasted_iota(jnp.int32, (tile, n), 0) + (base + i)
            hot = jnp.where(place == ids_ref[...], 1.0, 0.0).astype(BF16)
            both = dot(hot, pair_ref[...])
            out_ref[i : i + tile, :] = both[:, :emb] + both[:, emb:]


def table_sums(core, ids, grads, rows):
    n, emb = grads.shape
    half = rows // 2

    def whole(shape):
        return pl.BlockSpec(shape, lambda i, c: (0, 0))

    return pl.pallas_call(
        table_kernel,
        out_shape=[jax.ShapeDtypeStruct((half, emb), F32)] * 2,
        grid_spec=pltpu.PrefetchScalarGridSpec(
            num_scalar_prefetch=1,
            grid=(1,),
            in_specs=[whole((1, n)), whole((n, emb))],
            out_specs=[whole((half, emb))] * 2,
            scratch_shapes=[pltpu.VMEM((n, 2 * emb), BF16)],
        ),
        compiler_params=params(40 * MIB),
        cost_estimate=cost(2 * 10**9, 2 * MIB),
        name="table_sums",
    )(core, ids, grads)


def place_kernel(code_ref, *refs, blocks, pieces):
    n_in = sum(pieces)
    cross_ref, top_ref, sem = refs[n_in], refs[n_in + 1], refs[n_in + 2]
    n = cross_ref.shape[0] // blocks
    half = cross_ref.shape[1] // 2
    targets = [cross_ref.at[:, pl.ds(0, half)], cross_ref.at[:, pl.ds(half, half)], top_ref]
    copies, k = [], 0
    for colour, target in enumerate(targets):
        r = 0
        for _ in range(pieces[colour]):
            for i in range(0, refs[k].shape[0], n):
                at = pl.multiple_of((code_ref[colour] ^ r) * n, n)
                copies.append(
                    pltpu.make_async_copy(
                        refs[k].at[pl.ds(i, n)], target.at[pl.ds(at, n)], sem.at[len(copies)]
                    )
                )
                copies[-1].start()
                r += 1
            k += 1
    for copy in copies:
        copy.wait()


def place(codes, pieces, blocks):
    a, _, c = (p[0] for p in pieces)
    rows = sum(v.shape[0] for v in pieces[0])
    flat = [v for p in pieces for v in p]
    return pl.pallas_call(
        functools.partial(place_kernel, blocks=blocks, pieces=[len(p) for p in pieces]),
        out_shape=[
            jax.ShapeDtypeStruct((rows, 2 * a.shape[1]), F32),
            jax.ShapeDtypeStruct((rows, c.shape[1]), F32),
        ],
        in_specs=[pl.BlockSpec(memory_space=pltpu.SMEM)]
        + [pl.BlockSpec(memory_space=pltpu.VMEM)] * len(flat),
        out_specs=[pl.BlockSpec(memory_space=pl.ANY)] * 2,
        scratch_shapes=[pltpu.SemaphoreType.DMA((3 * blocks,))],
        compiler_params=params(PLACE_LIMIT),
        name="place",
    )(codes, *flat)


def tie(*values):
    return lax.optimization_barrier(values)


def halves(v):
    h = v.shape[0] // 2
    return v[:h], v[h:]


def on_device(
    sizes,
    table,
    cross_weight,
    cross_bias,
    top_weight,
    top_bias,
    out_weight,
    wanted,
    slots,
    lengths,
    logit_grad,
):
    emb = table.shape[1]
    width, top = top_weight.shape
    n_dp, n_shard = sizes["dp"].bit_length() - 1, sizes["shard"].bit_length() - 1
    n_y = n_shard // 2
    core = ("dp", 0)
    along_x = [("dp", k) for k in range(1, n_dp)]
    along_y = [("shard", k) for k in range(n_y)]
    along_z = [("shard", k) for k in range(n_y, n_shard)]
    order_a = [core] + along_x + along_y + along_z
    order_b = [core] + along_y + along_x + along_z
    order_c = [core] + along_z + along_x + along_y
    smallest = 16
    depth = min(n_dp + n_shard, (width // smallest).bit_length() - 1)
    blocks = 1 << depth
    position = {axis: lax.axis_index(axis) for axis in sizes}

    def bit(step):
        return (position[step[0]] >> step[1]) & 1

    def code(steps):
        total = jnp.int32(0)
        for step in steps[:depth]:
            total = total * 2 + bit(step)
        return total.astype(jnp.int32)

    def swap(v, step):
        axis, k = step
        return lax.ppermute(v, axis, [(i, i ^ (1 << k)) for i in range(sizes[axis])])

    def scatter(v, step, t):
        if t >= depth:
            return v + swap(v, step)
        keep, send = v if isinstance(v, tuple) else halves(v)
        return keep + swap(send, step)

    def spread(v, step, t):
        return v if t >= depth else jnp.concatenate([v, swap(v, step)])

    codes = jnp.stack([code(c) for c in (order_a, order_b, order_c)])
    my_core = bit(core).astype(jnp.int32).reshape(1)

    requests = wanted[0]
    served = lax.all_to_all(requests, "shard", split_axis=0, concat_axis=0, tiled=True)
    ids = served.reshape(-1)
    sent = gather_rows(table, ids).reshape(requests.shape + (emb,))
    cache = lax.all_to_all(sent, "shard", split_axis=0, concat_axis=0, tiled=True)
    rows = cache.reshape(-1, emb)

    hot = multi_hot(slots.transpose(1, 2, 0), lengths.T, rows.shape[0])
    logits, small_top, x0, y, dz, kc, sc = forward(
        codes, rows, hot, cross_weight.T, top_weight.T,
        cross_bias[:, None], top_bias[:, None], out_weight[:, None], logit_grad[None, :], blocks,
    )
    c = scatter((kc, sc), core, 0)
    small_cross, dyb, dxa, ka, sa, kb, sb = backward(codes, x0, y, dz, top_weight, blocks)
    small = jnp.concatenate([small_cross, small_top], axis=1)

    a = scatter((ka, sa), core, 0)
    b = scatter((kb, sb), core, 0)
    small = small + swap(small, core)
    a, b, c, small = tie(a, b, c, small)
    flat = len(along_x) + len(along_y)
    last = flat + len(along_z)
    c_steps = list(enumerate(order_c))[1:]
    c_at = {t: [] for t in range(1, last + 1)}
    for k, item in enumerate(c_steps):
        c_at[min(last, (1, 3, 4, 4)[k] if last == 4 else k + 1)].append(item)
    slot_grads = slot_gradients(dxa, cross_weight, dyb, hot).reshape(cache.shape)
    ab = None
    for t in range(1, last + 1):
        if t <= flat:
            a = scatter(a, order_a[t], t)
            b = scatter(b, order_b[t], t)
        else:
            if ab is None:
                ab = jnp.concatenate([a, b], axis=1)
            ab = scatter(ab, order_a[t], t)
        small = small + swap(small, order_a[t])
        for k, step in c_at[t]:
            c = scatter(c, step, k)
        tied = ([a, b] if ab is None else [ab]) + [small] + ([c] if c_at[t] else [])
        if t == 1:
            tied.append(slot_grads)
        tied = list(tie(*tied))
        if t == 1:
            slot_grads = tied.pop()
        if c_at[t]:
            c = tied.pop()
        small = tied.pop()
        if ab is None:
            a, b = tied
        else:
            (ab,) = tied
        if t == 1:
            returned = lax.all_to_all(slot_grads, "shard", split_axis=0, concat_axis=0, tiled=True)

    ab, c, returned = tie(ab, c, returned)
    keep, send = table_sums(my_core, ids[None, :], returned.reshape(-1, emb), table.shape[0])
    part = keep + swap(send, core)

    early = along_x + along_y if last == 4 else []
    for t in reversed(range(flat + 1, last + 1)):
        ab = spread(ab, order_a[t], t)
        if t == last:
            for k, step in reversed(c_steps):
                if step in early:
                    c = spread(c, step, k)
            ab, c, part = tie(ab, c, part)
            for step in along_x:
                part = part + swap(part, step)
        else:
            (ab,) = tie(ab)
    a, b = ab[:, : width // 2], ab[:, width // 2 :]
    late = [(k, step) for k, step in reversed(c_steps) if step not in early]
    for k, step in late[:-1]:
        c = spread(c, step, k)
    for t in reversed(range(2, flat + 1)):
        a, b = spread(a, order_a[t], t), spread(b, order_b[t], t)
    a, b, c, part = tie(a, b, c, part)
    other = swap(part, core)
    pieces = []
    for v, step in ((a, order_a[1]), (b, order_b[1]), (c, order_c[1])):
        pieces.append([v, swap(v, step)])
    for p in pieces:
        p += [swap(v, core) for v in p]
    g_cross, g_top = place(codes, pieces, blocks)
    first = my_core[0] == 0
    table_grad = jnp.concatenate([jnp.where(first, part, other), jnp.where(first, other, part)])
    small = small[0]
    return (
        logits[0], g_cross, g_top, small[:width], small[width : width + top],
        small[width + top :], table_grad,
    )


def solution(mesh):
    placed = (
        P("shard", None),
        P(),
        P(),
        P(),
        P(),
        P(),
        P(("dp", "shard"), None, None),
        P(("dp", "shard"), None, None),
        P(("dp", "shard"), None),
        P(("dp", "shard")),
    )
    return jax.shard_map(
        functools.partial(on_device, dict(mesh.shape)),
        mesh=mesh,
        in_specs=placed,
        out_specs=(P(("dp", "shard")), P(), P(), P(), P(), P(), P("shard", None)),
        check_vma=False,
    )
```
